32 devices in a mesh: dp: 8 (over z, y), section: 2 (over core), tensor: 2 (over x).
Axes of the slice: x: 2, y: 2, z: 4, core: 2. Of those that a mesh axis runs over, the one named last changes fastest.
Arguments:
- tokens: bfloat16 [128, 32, 1024], P('dp'), may hold values from -6 to 6
- counts: int32 [128], replicated, may hold values from 8 to 32, as said below
- assign: int32 [128], replicated, may hold values from 0 to 127, as said below
- qkv_weight: bfloat16 [2, 1024, 3, 1024], P('section', 'dp', None, 'tensor'), may hold values from -0.9375 to 0.9375
- out_weight: bfloat16 [2, 1024, 1024], P('section', 'dp'), may hold values from -0.1875 to 0.1875
- up_weight: bfloat16 [2, 1024, 4096], P('section', 'dp', 'tensor'), may hold values from -0.1875 to 0.1875
- up_bias: bfloat16 [2, 4096], P('section', 'tensor'), may hold values from -3 to 3
- down_weight: bfloat16 [2, 4096, 1024], P('section', 'tensor', 'dp'), may hold values from -0.09375 to 0.09375
- attn_gain: bfloat16 [2, 1024], P('section'), may hold values from 0.25 to 1.75
- mlp_gain: bfloat16 [2, 1024], P('section'), may hold values from 0.25 to 1.75
- final_gain: bfloat16 [1024], replicated, may hold values from 0.25 to 1.75
Outputs:
- encoded: bfloat16 [128, 32, 1024], P('dp', 'section', 'tensor')
The draws below stay inside these ranges and needn't reach their ends.
Inputs may be any that keep to these rules, and one draw needn't show every extreme that they name: `counts`: every count is at least 8, and in every draw some image has all 32 slots live. assign is a permutation of the images. Slot j belongs to data group j // 16, so every data group receives 16 images; within one data group's slots the images stand in increasing order. Images of data group g are tokens rows g * 16 to (g + 1) * 16 - 1. No data group hands more than 2 images to one data group (itself included), and in every draw some pair of data groups exchanges exactly 2. Every data group receives some image from the data group half the axis away.
All inputs are finite; a program needn't handle non-finite values.
Results may differ from the reference program's by a relative error of at most 0.024.
The reference program's roundings to bfloat16 on the way count: a program that leaves them out, or rounds other values in their place, can miss the bound.
Values may be sent and summed in bfloat16 or wider, within the bound.
A program may use at most 128 MiB of HBM per device.

```python
import jax
import jax.numpy as jnp
from jax import lax

D = 1024
FF = 4096
BLOCK = 32
IMG_DEV = 16
HEAD_DIM = 64
LAYERS = 2
IMAGES = 128
CAP = 2
N_TENSOR = 2


def draw_counts(key, part):
    first_key, second_key = jax.random.split(jax.random.fold_in(key, 7))
    values = jax.random.randint(first_key, (IMAGES,), BLOCK // 4, BLOCK + 1)
    chosen_image = jax.random.randint(second_key, (), 0, IMAGES)
    return jnp.where(jnp.arange(IMAGES) == chosen_image, BLOCK, values).astype(jnp.int32)


def draw_assign(key, part):
    groups = IMAGES // IMG_DEV
    base_key = jax.random.fold_in(key, 11)
    order_key, shuffle_key = jax.random.split(base_key, 2)
    offsets_pool = jnp.repeat(jnp.arange(groups, dtype=jnp.int32), CAP)
    favoured = groups // 2
    order_score = jax.random.permutation(order_key, groups * CAP).astype(jnp.int32)
    order_score = jnp.where(offsets_pool == favoured, order_score - groups * CAP, order_score)
    taken = offsets_pool[jnp.argsort(order_score)[:IMG_DEV]]
    offsets = jax.random.permutation(shuffle_key, taken)
    group_numbers = jnp.arange(groups, dtype=jnp.int32)
    local_order = jax.vmap(lambda number: jax.random.permutation(jax.random.fold_in(base_key, 100 + number), IMG_DEV))(group_numbers)
    target_group = (group_numbers[:, None] + offsets[None, :]) % groups
    image_index = group_numbers[:, None] * IMG_DEV + local_order
    destination = jnp.zeros((IMAGES,), jnp.int32).at[image_index.reshape(-1)].set(target_group.reshape(-1).astype(jnp.int32))
    return jnp.argsort(destination * IMAGES + jnp.arange(IMAGES, dtype=jnp.int32)).astype(jnp.int32)


def draw_qkv_weight(key, part):
    values = jnp.clip(jax.random.normal(jax.random.fold_in(key, 13), (LAYERS, D, 3, D), jnp.float32), -5.0, 5.0) * D ** (-0.5)
    return values.astype(jnp.bfloat16)


def steps_of(stream_key, dims, pieces, low, largest):
    gain, own = 1.0, jax.random.fold_in(stream_key, 6)
    for dim, parts in pieces:
        steps = jnp.exp(jax.random.uniform(jax.random.fold_in(own, dim), (parts,), jnp.float32, low / len(pieces), largest / len(pieces)))
        gain = gain * jnp.repeat(steps, dims[dim] // parts).reshape([-1 if axis == dim else 1 for axis in range(len(dims))])
    return gain


def bell_draw(key, extent, scale, limit, pieces=(), kind=jnp.bfloat16):
    level = steps_of(key, extent, pieces, -0.22, 0.18) if pieces else 1.0
    values = jax.random.normal(key, extent, jnp.float32) * scale * level
    return jnp.minimum(jnp.maximum(values, -limit), limit).astype(kind)


def setup_inputs(seed: int = 0) -> dict:
    streams_of = jax.random.split(jax.random.key(seed), 12)
    return {
        "tokens": bell_draw(streams_of[0], (IMAGES, BLOCK, D), 1.0, 6.0, ((0, 8),)),
        "counts": draw_counts(jax.random.fold_in(streams_of[11], 71), 0),
        "assign": draw_assign(jax.random.fold_in(streams_of[11], 71), 0),
        "qkv_weight": draw_qkv_weight(jax.random.fold_in(streams_of[11], 71), 0),
        "out_weight": bell_draw(streams_of[4], (LAYERS, D, D), D ** -0.5, 0.1875, ((0, 2), (1, 8))),
        "up_weight": bell_draw(streams_of[5], (LAYERS, D, FF), D ** -0.5, 0.1875, ((0, 2), (1, 8), (2, 2))),
        "up_bias": bell_draw(streams_of[6], (LAYERS, FF), 0.5, 3.0, ((0, 2), (1, 2))),
        "down_weight": bell_draw(streams_of[7], (LAYERS, FF, D), FF ** -0.5, 0.09375, ((0, 2), (1, 2), (2, 8))),
        "attn_gain": jnp.clip(1.0 + 0.15 * jax.random.normal(streams_of[8], (LAYERS, D), jnp.float32), 0.25, 1.75).astype(jnp.bfloat16),
        "mlp_gain": jnp.clip(1.0 + 0.15 * jax.random.normal(streams_of[9], (LAYERS, D), jnp.float32), 0.25, 1.75).astype(jnp.bfloat16),
        "final_gain": jnp.clip(1.0 + 0.15 * jax.random.normal(streams_of[10], (D,), jnp.float32), 0.25, 1.75).astype(jnp.bfloat16),
    }


epsilon = 1e-06

def layer_norm(values, gain_vector):
    average = lax.optimization_barrier(jnp.mean(values, axis=-1, keepdims=True))
    centred = values - average
    spread = lax.optimization_barrier(jnp.mean(centred * centred, axis=-1, keepdims=True))
    return centred * lax.rsqrt(spread + epsilon) * gain_vector.astype(jnp.float32)

def attend(normed, w_merged, live_count, head_dim):
    row_count = normed.shape[0]
    merged = jnp.dot(normed, w_merged.reshape(w_merged.shape[0], -1), preferred_element_type=jnp.float32)
    merged = merged.reshape(row_count, 3, -1, head_dim)
    scores = jnp.einsum('qhd,khd->hqk', merged[:, 0], merged[:, 1], precision=lax.Precision.HIGHEST) * head_dim ** (-0.5)
    visible = jnp.arange(row_count) < live_count
    scores = jnp.where(visible[None, None, :], scores, -1e+30)
    weights = jax.nn.softmax(scores, axis=-1)
    mixed = jnp.einsum('hqk,khd->qhd', weights, merged[:, 2], precision=lax.Precision.HIGHEST)
    return mixed.reshape(row_count, -1).astype(jnp.bfloat16)

def reference(tokens, counts, assign, qkv_weight, out_weight, up_weight, up_bias, down_weight, attn_gain, mlp_gain, final_gain):
    stream = tokens[assign]
    live_counts = counts[assign]
    images, block_rows, model_width = stream.shape
    quarter = FF // N_TENSOR

    def one_layer(stream, layer_weights):
        qkv_full, out_full, up_full, bias_row, down_full, gain_attn, gain_mlp = layer_weights
        normed = layer_norm(stream.astype(jnp.float32), gain_attn).astype(jnp.bfloat16)
        head_out = jax.vmap(lambda image_rows, live_count: attend(image_rows, qkv_full, live_count, HEAD_DIM))(normed, live_counts)
        flat = head_out.reshape(images * block_rows, model_width)
        middle = stream.reshape(-1, model_width).astype(jnp.float32) + jnp.dot(flat, out_full, preferred_element_type=jnp.float32)
        normed_mlp = layer_norm(middle, gain_mlp).astype(jnp.bfloat16)
        hidden = jax.nn.gelu(jnp.dot(normed_mlp, up_full, preferred_element_type=jnp.float32) + bias_row.astype(jnp.float32), approximate=False).astype(jnp.bfloat16)
        summed = jnp.zeros_like(middle)
        for shard_index in range(N_TENSOR):
            lower = shard_index * quarter
            partial_value = jnp.dot(hidden[:, lower:lower + quarter], down_full[lower:lower + quarter], preferred_element_type=jnp.float32)
            rounded = lax.optimization_barrier(partial_value.astype(jnp.bfloat16))
            summed = summed + rounded.astype(jnp.float32)
        updated = (middle + summed).astype(jnp.bfloat16)
        return (updated.reshape(images, block_rows, model_width), None)
    stream, _ = lax.scan(one_layer, stream, (qkv_weight, out_weight, up_weight, up_bias, down_weight, attn_gain, mlp_gain))
    visible = jnp.arange(block_rows)[None, :, None] < live_counts[:, None, None]
    normed_out = layer_norm(stream.astype(jnp.float32), final_gain)
    return jnp.where(visible, normed_out, 0.0).astype(jnp.bfloat16)
```

```python
import functools

import jax
import jax.numpy as jnp
from jax import lax
from jax.experimental import pallas as pl
from jax.experimental.pallas import tpu as pltpu
from jax.sharding import PartitionSpec as P

HEAD_DIM = 64
CHUNK = 128
TILE = 256
epsilon = 1e-06
BF = jnp.bfloat16
F32 = jnp.float32


def normalised(values, gain_row):
    average = jnp.mean(values, axis=-1, keepdims=True)
    centred = values - average
    spread = jnp.mean(centred * centred, axis=-1, keepdims=True)
    return centred * lax.rsqrt(spread + epsilon) * gain_row


def encoder(
    groups,
    cap_rows,
    tok,
    select,
    pick,
    mask,
    bias,
    gain_attn,
    gain_mlp,
    gain_final,
    w_qkv,
    w_out,
    w_up,
    w_down,
    o_ref,
    g_qkv,
    g_out,
    g_up,
    g_down,
    outgoing,
    received,
    x,
    normed,
    merged,
    ho_mine,
    ho_other,
    mid,
    hidden,
    p_mine,
    p_other,
    stream,
    fin,
    tok_ss,
    tok_rs,
    own_s,
    line_up,
    line_down,
    line_rs,
    pair_ss,
    pair_rs,
    ho_ss,
    ho_rs,
    p_ss,
    p_rs,
    x_ss,
    x_rs,
    fin_s,
    go_sem,
):
    me = lax.axis_index("dp")
    section = lax.axis_index("section")
    tensor = lax.axis_index("tensor")
    half = groups // 2
    high, low = me // 2, me % 2
    rows, width = tok.shape
    quarter = ho_mine.shape[1]
    images, section_rows, _ = o_ref.shape
    block = fin.shape[1]
    above = {"dp": jnp.minimum(high + 1, half - 1) * 2 + low}
    below = {"dp": jnp.maximum(high - 1, 0) * 2 + low}
    pair = {"dp": high * 2 + 1 - low}
    beside = {"tensor": 1 - tensor}
    partner = {"section": 1 - section}

    def remote(src, dst, ss, rs, device):
        return pltpu.make_async_remote_copy(
            src_ref=src,
            dst_ref=dst,
            send_sem=ss,
            recv_sem=rs,
            device_id=device,
            device_id_type=pl.DeviceIdType.MESH,
        )

    barrier = pltpu.get_barrier_semaphore()
    for step in range(1, groups):
        pl.semaphore_signal(
            barrier,
            inc=1,
            device_id={"dp": (me + step) % groups},
            device_id_type=pl.DeviceIdType.MESH,
        )
    for device in (beside, partner):
        pl.semaphore_signal(
            barrier, inc=1, device_id=device, device_id_type=pl.DeviceIdType.MESH
        )
    pl.semaphore_wait(barrier, groups + 1)

    weights = ((w_qkv, g_qkv), (w_out, g_out), (w_up, g_up), (w_down, g_down))
    narrow = len(g_down.shape) == 3

    def piece(which, number):
        source, whole = weights[which]
        if which < 3:
            size = source.shape[0]
            return whole.at[pl.ds(pl.multiple_of(number * size, size), size), :]
        size = source.shape[1]
        if narrow:
            return whole.at[number]
        return whole.at[:, pl.ds(pl.multiple_of(number * size, size), size)]

    def slot(buffer, number):
        return buffer.at[pl.ds(pl.multiple_of(number * cap_rows, cap_rows), cap_rows), :]

    first = section == 0
    second = section == 1

    def token_copy(step):
        peer = (me + step) % groups
        return remote(
            slot(outgoing, peer), slot(received, me), tok_ss.at[peer], tok_rs.at[me], {"dp": peer}
        )

    def token_arrival(step):
        peer = (me + step) % groups
        return remote(
            slot(outgoing, peer), slot(received, peer), tok_ss.at[peer], tok_rs.at[peer], {"dp": peer}
        )

    own_tokens = pltpu.make_async_copy(slot(outgoing, me), slot(received, me), tok_ss.at[me])

    @pl.when(first)
    def _():
        slots = outgoing.shape[0]

        @pl.loop(0, width // TILE)
        def _(tile):
            columns = pl.ds(pl.multiple_of(tile * TILE, TILE), TILE)
            outgoing[:, columns] = jnp.dot(
                select[...], tok[:, columns], preferred_element_type=F32
            ).astype(BF)

        for step in range(1, groups):
            token_copy(step).start()
        own_tokens.start()

    @pl.when(second)
    def _():
        pl.semaphore_wait(go_sem, 1)

    owns = []
    for which in range(4):
        own = pltpu.make_async_copy(weights[which][0], piece(which, me), own_s.at[which])
        own.start()
        owns.append(own)

    def up_copy(which, source_high, src):
        return remote(
            src,
            piece(which, source_high * 2 + low),
            line_up.at[which, source_high],
            line_rs.at[which, source_high],
            above,
        )

    def down_copy(which, source_high, src):
        return remote(
            src,
            piece(which, source_high * 2 + low),
            line_down.at[which, source_high],
            line_rs.at[which, source_high],
            below,
        )

    def pair_copy(which, source_high, src):
        return remote(
            src,
            piece(which, source_high * 2 + low),
            pair_ss.at[which, source_high],
            pair_rs.at[which, source_high],
            pair,
        )

    has_above = high < half - 1
    has_below = high > 0
    for which in range(4):
        source = weights[which][0]

        @pl.when(has_above)
        def _():
            up_copy(which, high, source).start()

        @pl.when(has_below)
        def _():
            down_copy(which, high, source).start()

        pair_copy(which, high, source).start()

    def relay(which, back):
        lower = high - back

        @pl.when(lower >= 0)
        def _():
            src = piece(which, lower * 2 + low)
            arriving = up_copy(which, lower, src)
            arriving.wait_recv()

            @pl.when(has_above)
            def _():
                up_copy(which, lower, src).start()

            pair_copy(which, lower, src).start()

        upper = high + back

        @pl.when(upper < half)
        def _():
            src = piece(which, upper * 2 + low)
            arriving = down_copy(which, upper, src)
            arriving.wait_recv()

            @pl.when(has_below)
            def _():
                down_copy(which, upper, src).start()

            pair_copy(which, upper, src).start()

    for back in range(1, half):
        for which in range(4):
            relay(which, back)

    @pl.when(first)
    def _():
        pl.semaphore_signal(
            go_sem, inc=1, device_id=partner, device_id_type=pl.DeviceIdType.MESH
        )

    def gathered(which):
        owns[which].wait()
        for source_high in range(half):
            other = piece(which, source_high * 2 + 1 - low)
            remote(
                other, other, pair_ss.at[which, source_high], pair_rs.at[which, source_high], pair
            ).wait_recv()

    chunks = rows // CHUNK

    def chunk_rows(chunk):
        return pl.ds(pl.multiple_of(chunk * CHUNK, CHUNK), CHUNK)

    def stream_copy(part):
        at = pl.ds(part * TILE, TILE)
        return remote(
            stream.at[at, :], x.at[at, :], x_ss.at[part], x_rs.at[part], partner
        )

    parts = rows // TILE

    @pl.when(first)
    def _():
        for step in range(1, groups):
            token_arrival(step).wait_recv()
        own_tokens.wait()

        @pl.loop(0, width // TILE)
        def _(tile):
            columns = pl.ds(pl.multiple_of(tile * TILE, TILE), TILE)
            x[:, columns] = jnp.dot(
                pick[...], received[:, columns], preferred_element_type=F32
            ).astype(BF)

    for which in range(4):
        gathered(which)

    @pl.when(second)
    def _():
        for part in range(parts):
            stream_copy(part).wait_recv()

    @pl.loop(0, chunks)
    def _(chunk):
        at = chunk_rows(chunk)
        normed[at, :] = normalised(x[at, :].astype(F32), gain_attn[...]).astype(BF)

    @pl.loop(0, merged.shape[1] // TILE)
    def _(tile):
        columns = pl.ds(pl.multiple_of(tile * TILE, TILE), TILE)
        merged[:, columns] = jnp.dot(normed[...], g_qkv[:, columns], preferred_element_type=F32)

    lanes = 2 * HEAD_DIM
    lane_of = lax.broadcasted_iota(jnp.int32, (CHUNK, lanes), 1)
    contract = (((1,), (1,)), ((), ()))

    def head_copy(chunk):
        at = chunk_rows(chunk)
        return remote(
            ho_mine.at[at, :], ho_other.at[at, :], ho_ss.at[chunk], ho_rs.at[chunk], beside
        )

    @pl.loop(0, chunks)
    def _(chunk):
        at = chunk_rows(chunk)
        hidden_keys = mask[chunk]
        for two in range(quarter // lanes):
            q = merged[at, two * lanes : (two + 1) * lanes]
            k = merged[at, quarter + two * lanes : quarter + (two + 1) * lanes]
            v = merged[at, 2 * quarter + two * lanes : 2 * quarter + (two + 1) * lanes].astype(BF)
            k_top = k.astype(BF)
            k_rest = (k - k_top.astype(F32)).astype(BF)
            outs = []
            for head in range(2):
                mine = (lane_of < HEAD_DIM) if head == 0 else (lane_of >= HEAD_DIM)
                q_head = jnp.where(mine, q, 0.0)
                q_top = q_head.astype(BF)
                q_rest = (q_head - q_top.astype(F32)).astype(BF)
                scores = (
                    lax.dot_general(q_top, k_top, contract, preferred_element_type=F32)
                    + lax.dot_general(q_top, k_rest, contract, preferred_element_type=F32)
                    + lax.dot_general(q_rest, k_top, contract, preferred_element_type=F32)
                ) * HEAD_DIM ** (-0.5)
                scores = scores + hidden_keys
                scores = scores - jnp.max(scores, axis=-1, keepdims=True)
                powers = jnp.exp(scores)
                total = jnp.sum(powers, axis=-1, keepdims=True)
                mixed = jnp.dot(powers.astype(BF), v, preferred_element_type=F32)
                outs.append(mixed / total)
            ho_mine[at, two * lanes : (two + 1) * lanes] = jnp.where(
                lane_of < HEAD_DIM, outs[0], outs[1]
            ).astype(BF)
        head_copy(chunk).start()

    @pl.loop(0, chunks)
    def _(chunk):
        head_copy(chunk).wait()

    mine_rows = pl.ds(pl.multiple_of(tensor * quarter, quarter), quarter)
    other_rows = pl.ds(pl.multiple_of((1 - tensor) * quarter, quarter), quarter)

    @pl.loop(0, width // TILE)
    def _(tile):
        columns = pl.ds(pl.multiple_of(tile * TILE, TILE), TILE)
        mid[:, columns] = (
            x[:, columns].astype(F32)
            + jnp.dot(ho_mine[...], g_out[mine_rows, columns], preferred_element_type=F32)
            + jnp.dot(ho_other[...], g_out[other_rows, columns], preferred_element_type=F32)
        )

    @pl.loop(0, chunks)
    def _(chunk):
        at = chunk_rows(chunk)
        normed[at, :] = normalised(mid[at, :], gain_mlp[...]).astype(BF)

    @pl.loop(0, hidden.shape[1] // TILE)
    def _(tile):
        columns = pl.ds(pl.multiple_of(tile * TILE, TILE), TILE)
        raised = (
            jnp.dot(normed[...], g_up[:, columns], preferred_element_type=F32) + bias[:, columns]
        )
        hidden[:, columns] = (raised * (1.0 + lax.erf(raised * (0.5**0.5))) * 0.5).astype(BF)

    def partial_copy(part):
        at = pl.ds(part * TILE, TILE)
        return remote(p_mine.at[at, :], p_other.at[at, :], p_ss.at[part], p_rs.at[part], beside)

    for part in range(parts):
        at = pl.ds(part * TILE, TILE)

        @pl.loop(0, width // TILE)
        def _(tile):
            columns = pl.ds(pl.multiple_of(tile * TILE, TILE), TILE)
            if narrow:
                count = TILE // g_down.shape[2]
                product = jnp.concatenate(
                    [
                        jnp.dot(
                            hidden[at, :], g_down[tile * count + i], preferred_element_type=F32
                        )
                        for i in range(count)
                    ],
                    axis=1,
                )
            else:
                product = jnp.dot(hidden[at, :], g_down[:, columns], preferred_element_type=F32)
            p_mine[at, columns] = product.astype(BF)

        partial_copy(part).start()

    for part in range(parts):
        at = pl.ds(part * TILE, TILE)
        partial_copy(part).wait()
        stream[at, :] = (
            mid[at, :] + (p_mine[at, :].astype(F32) + p_other[at, :].astype(F32))
        ).astype(BF)

        @pl.when(first)
        def _():
            stream_copy(part).start()

    result = remote(
        fin.at[:, pl.ds(0, section_rows), :], o_ref, fin_s.at[0], fin_s.at[1], partner
    )

    @pl.when(second)
    def _():
        per = CHUNK // block
        own_columns = pl.ds(pl.multiple_of(tensor * quarter, quarter), quarter)

        @pl.loop(0, chunks)
        def _(chunk):
            at = chunk_rows(chunk)
            values = stream[at, :].astype(F32)
            average = jnp.mean(values, axis=-1, keepdims=True)
            centred = values - average
            scale = lax.rsqrt(jnp.mean(centred * centred, axis=-1, keepdims=True) + epsilon)
            piece_values = (
                (stream[at, own_columns].astype(F32) - average) * scale * gain_final[:, own_columns]
            )
            fin[pl.ds(chunk * per, per)] = piece_values.astype(BF).reshape(per, block, quarter)

        result.start()
        o_ref[...] = fin[:, section_rows:, :]
        result.wait_send()

    @pl.when(first)
    def _():
        for part in range(parts):
            stream_copy(part).wait_send()
        for step in range(1, groups):
            token_copy(step).wait_send()
        result.wait_recv()

    for which in range(4):
        source = weights[which][0]
        for back in range(half):

            @pl.when(has_above & (high - back >= 0))
            def _():
                up_copy(which, high - back, source).wait_send()

            @pl.when(has_below & (high + back < half))
            def _():
                down_copy(which, high + back, source).wait_send()

            pair_copy(which, back, source).wait_send()


def local(
    tokens,
    counts,
    assign,
    qkv_weight,
    out_weight,
    up_weight,
    up_bias,
    down_weight,
    attn_gain,
    mlp_gain,
    final_gain,
):
    groups = lax.axis_size("dp")
    sections = lax.axis_size("section")
    tensor_ranks = lax.axis_size("tensor")
    images_dev, block, width = tokens.shape
    quarter = width // tensor_ranks
    capacity = (images_dev + groups - 1) // groups
    total_images = assign.shape[0]
    rows = images_dev * block
    slots = groups * capacity
    my_group = lax.axis_index("dp")
    numbers = jnp.arange(total_images, dtype=jnp.int32)
    matches = (assign[:, None] == numbers[None, :]).astype(jnp.int32)
    slot_of = jnp.sum(matches * numbers[:, None], axis=0)
    target = slot_of // images_dev
    source_group = numbers // images_dev
    earlier = (
        (source_group[:, None] == source_group[None, :])
        & (target[:, None] == target[None, :])
        & (numbers[None, :] < numbers[:, None])
    )
    rank_all = jnp.sum(earlier.astype(jnp.int32), axis=1)
    send_slot = lax.dynamic_slice_in_dim(
        target * capacity + rank_all, my_group * images_dev, images_dev
    )
    my_images = lax.dynamic_slice_in_dim(assign, my_group * images_dev, images_dev)
    chosen = (my_images[:, None] == numbers[None, :]).astype(jnp.int32)
    receive_slot = jnp.sum(chosen * (source_group * capacity + rank_all)[None, :], axis=1)
    live_counts = jnp.sum(chosen * counts[None, :], axis=1)
    within = jnp.tile(jnp.arange(block, dtype=jnp.int32), images_dev)
    buffer_rows = jnp.arange(slots * block, dtype=jnp.int32)
    send_rows = jnp.repeat(send_slot, block) * block + within
    receive_rows = jnp.repeat(receive_slot, block) * block + within
    select = (buffer_rows[:, None] == send_rows[None, :]).astype(BF)
    pick = (buffer_rows[None, :] == receive_rows[:, None]).astype(BF)
    per = CHUNK // block
    key_live = within.reshape(-1, CHUNK) < jnp.repeat(live_counts, block).reshape(-1, CHUNK)
    image_of = jnp.arange(CHUNK) // block
    visible = key_live[:, None, :] & (image_of[:, None] == image_of[None, :])[None]
    mask = jnp.where(visible, 0.0, -1e30).astype(F32)
    w_qkv = qkv_weight[0].reshape(qkv_weight.shape[1], -1)
    w_out, w_up, w_down = out_weight[0], up_weight[0], down_weight[0]
    units = w_up.shape[1]
    down_columns = w_down.shape[1]
    down_shape = (units, width) if down_columns % 128 == 0 else (groups, units, down_columns)
    half = groups // 2
    cap_rows = capacity * block
    vmem = pl.BlockSpec(memory_space=pltpu.VMEM)
    anywhere = pl.BlockSpec(memory_space=pl.ANY)
    dma = pltpu.SemaphoreType.DMA
    section_rows = block // sections
    encoded = pl.pallas_call(
        functools.partial(encoder, groups, cap_rows),
        out_shape=jax.ShapeDtypeStruct((images_dev, section_rows, quarter), BF),
        in_specs=[vmem] * 8 + [anywhere] * 4,
        out_specs=vmem,
        scratch_shapes=[
            pltpu.VMEM((width, w_qkv.shape[1]), BF),
            pltpu.VMEM((width, width), BF),
            pltpu.VMEM((width, units), BF),
            pltpu.VMEM(down_shape, BF),
            pltpu.VMEM((slots * block, width), BF),
            pltpu.VMEM((slots * block, width), BF),
            pltpu.VMEM((rows, width), BF),
            pltpu.VMEM((rows, width), BF),
            pltpu.VMEM((rows, w_qkv.shape[1]), F32),
            pltpu.VMEM((rows, quarter), BF),
            pltpu.VMEM((rows, quarter), BF),
            pltpu.VMEM((rows, width), F32),
            pltpu.VMEM((rows, units), BF),
            pltpu.VMEM((rows, width), BF),
            pltpu.VMEM((rows, width), BF),
            pltpu.VMEM((rows, width), BF),
            pltpu.VMEM((images_dev, block, quarter), BF),
            dma((groups,)),
            dma((groups,)),
            dma((4,)),
            dma((4, half)),
            dma((4, half)),
            dma((4, half)),
            dma((4, half)),
            dma((4, half)),
            dma((rows // CHUNK,)),
            dma((rows // CHUNK,)),
            dma((rows // TILE,)),
            dma((rows // TILE,)),
            dma((rows // TILE,)),
            dma((rows // TILE,)),
            dma((2,)),
            pltpu.SemaphoreType.REGULAR,
        ],
        compiler_params=pltpu.CompilerParams(
            collective_id=0, has_side_effects=True, vmem_limit_bytes=60 * 1024 * 1024
        ),
    )(
        tokens.reshape(rows, width),
        select,
        pick,
        mask,
        up_bias[0].astype(F32)[None],
        attn_gain[0].astype(F32)[None],
        mlp_gain[0].astype(F32)[None],
        final_gain.astype(F32)[None],
        w_qkv,
        w_out,
        w_up,
        w_down,
    )
    row_numbers = lax.axis_index("section") * section_rows + jnp.arange(section_rows)
    alive = row_numbers[None, :, None] < live_counts[:, None, None]
    return jnp.where(alive, encoded, jnp.zeros_like(encoded))


def solution(mesh):
    in_specs = (
        P("dp", None, None),
        P(),
        P(),
        P("section", "dp", None, "tensor"),
        P("section", "dp", None),
        P("section", "dp", "tensor"),
        P("section", "tensor"),
        P("section", "tensor", "dp"),
        P("section", None),
        P("section", None),
        P(),
    )
    out_specs = P("dp", "section", "tensor")
    return jax.shard_map(local, mesh=mesh, in_specs=in_specs, out_specs=out_specs, check_vma=False)
```

```python
import functools

import jax
import jax.numpy as jnp
from jax import lax
from jax.experimental import pallas as pl
from jax.experimental.pallas import tpu as pltpu
from jax.sharding import PartitionSpec as P

HEAD_DIM = 64
CHUNK = 128
TILE = 256
epsilon = 1e-06
BF = jnp.bfloat16
F32 = jnp.float32


def normalised(values, gain_row):
    average = jnp.mean(values, axis=-1, keepdims=True)
    centred = values - average
    spread = jnp.mean(centred * centred, axis=-1, keepdims=True)
    return centred * lax.rsqrt(spread + epsilon) * gain_row


def encoder(
    groups,
    cap_rows,
    tok,
    select,
    pick,
    mask,
    bias,
    gain_attn,
    gain_mlp,
    gain_final,
    w_qkv,
    w_out,
    w_up,
    w_down,
    o_ref,
    g_qkv,
    g_out,
    g_up,
    g_down,
    outgoing,
    received,
    x,
    normed,
    merged,
    ho_mine,
    ho_other,
    mid,
    hidden,
    p_mine,
    p_other,
    stream,
    fin,
    tok_ss,
    tok_rs,
    own_s,
    line_up,
    line_down,
    line_rs,
    pair_ss,
    pair_rs,
    ho_ss,
    ho_rs,
    p_ss,
    p_rs,
    x_ss,
    x_rs,
    fin_s,
    lend_ss,
    lend_rs,
    swap_s,
    go_sem,
):
    me = lax.axis_index("dp")
    section = lax.axis_index("section")
    tensor = lax.axis_index("tensor")
    half = groups // 2
    high, low = me // 2, me % 2
    rows, width = tok.shape
    quarter = ho_mine.shape[1]
    images, section_rows, _ = o_ref.shape
    block = fin.shape[1]
    above = {"dp": jnp.minimum(high + 1, half - 1) * 2 + low}
    below = {"dp": jnp.maximum(high - 1, 0) * 2 + low}
    pair = {"dp": high * 2 + 1 - low}
    beside = {"tensor": 1 - tensor}
    partner = {"section": 1 - section}

    def remote(src, dst, ss, rs, device):
        return pltpu.make_async_remote_copy(
            src_ref=src,
            dst_ref=dst,
            send_sem=ss,
            recv_sem=rs,
            device_id=device,
            device_id_type=pl.DeviceIdType.MESH,
        )

    barrier = pltpu.get_barrier_semaphore()
    for step in range(1, groups):
        pl.semaphore_signal(
            barrier,
            inc=1,
            device_id={"dp": (me + step) % groups},
            device_id_type=pl.DeviceIdType.MESH,
        )
    for device in (beside, partner):
        pl.semaphore_signal(
            barrier, inc=1, device_id=device, device_id_type=pl.DeviceIdType.MESH
        )
    pl.semaphore_wait(barrier, groups + 1)

    narrow = len(g_down.shape) == 3
    mine_columns = pl.ds(pl.multiple_of(tensor * quarter, quarter), quarter)
    sources = (w_qkv, w_out.at[:, mine_columns], w_up, w_down)
    wholes = (g_qkv, g_out, g_up, g_down)
    lent = (1, 2)

    def piece(which, number):
        source, whole = sources[which], wholes[which]
        if which < 3:
            size = source.shape[0]
            at = pl.ds(pl.multiple_of(number * size, size), size)
            return whole.at[at, mine_columns] if which == 1 else whole.at[at, :]
        if narrow:
            return whole.at[number]
        size = source.shape[1]
        return whole.at[:, pl.ds(pl.multiple_of(number * size, size), size)]

    def slot(buffer, number):
        return buffer.at[pl.ds(pl.multiple_of(number * cap_rows, cap_rows), cap_rows), :]

    first = section == 0
    second = section == 1

    def token_copy(step):
        peer = (me + step) % groups
        return remote(
            slot(outgoing, peer), slot(received, me), tok_ss.at[peer], tok_rs.at[me], {"dp": peer}
        )

    def token_arrival(step):
        peer = (me + step) % groups
        return remote(
            slot(outgoing, peer), slot(received, peer), tok_ss.at[peer], tok_rs.at[peer], {"dp": peer}
        )

    own_tokens = pltpu.make_async_copy(slot(outgoing, me), slot(received, me), tok_ss.at[me])

    def up_copy(which, source_high, src):
        return remote(
            src,
            piece(which, source_high * 2 + low),
            line_up.at[which, source_high],
            line_rs.at[which, source_high],
            above,
        )

    def down_copy(which, source_high, src):
        return remote(
            src,
            piece(which, source_high * 2 + low),
            line_down.at[which, source_high],
            line_rs.at[which, source_high],
            below,
        )

    def pair_copy(which, source_high, src):
        return remote(
            src,
            piece(which, source_high * 2 + low),
            pair_ss.at[which, source_high],
            pair_rs.at[which, source_high],
            pair,
        )

    has_above = high < half - 1
    has_below = high > 0
    in_lower = high < half // 2
    lends_above = has_above & (high + 1 >= half // 2)
    lends_below = has_below & (high - 1 < half // 2)
    lender = jnp.where(in_lower, high + 1, high - 1)

    owns = [
        pltpu.make_async_copy(sources[which], piece(which, me), own_s.at[which])
        for which in range(4)
    ]

    def send_own(which):
        source = sources[which]

        @pl.when(has_above)
        def _():
            up_copy(which, high, source).start()

        @pl.when(has_below)
        def _():
            down_copy(which, high, source).start()

        pair_copy(which, high, source).start()
        owns[which].start()

    def relay(which, back):
        lower = high - back

        @pl.when(lower >= 0)
        def _():
            src = piece(which, lower * 2 + low)
            up_copy(which, lower, src).wait_recv()

            @pl.when(has_above)
            def _():
                up_copy(which, lower, src).start()

            if which in lent:

                @pl.when(lower != lender)
                def _():
                    pair_copy(which, lower, src).start()

            else:
                pair_copy(which, lower, src).start()

        upper = high + back

        @pl.when(upper < half)
        def _():
            src = piece(which, upper * 2 + low)
            down_copy(which, upper, src).wait_recv()

            @pl.when(has_below)
            def _():
                down_copy(which, upper, src).start()

            if which in lent:

                @pl.when(upper != lender)
                def _():
                    pair_copy(which, upper, src).start()

            else:
                pair_copy(which, upper, src).start()

    def pair_arrival(which, source_high):
        other = piece(which, source_high * 2 + 1 - low)
        return remote(
            other, other, pair_ss.at[which, source_high], pair_rs.at[which, source_high], pair
        )

    def lend_copy(which, direction):
        other = piece(which, high * 2 + 1 - low)
        return remote(
            other,
            other,
            lend_ss.at[which, direction],
            lend_rs.at[which],
            below if direction == 0 else above,
        )

    def lend(which):
        pair_arrival(which, high).wait_recv()

        @pl.when(lends_below)
        def _():
            lend_copy(which, 0).start()

        @pl.when(lends_above)
        def _():
            lend_copy(which, 1).start()

    def gathered(which):
        owns[which].wait()
        for source_high in range(half):
            if which in lent:

                @pl.when((high != source_high) & (lender != source_high))
                def _():
                    pair_arrival(which, source_high).wait_recv()

            else:
                pair_arrival(which, source_high).wait_recv()
        if which in lent:
            borrowed = piece(which, lender * 2 + 1 - low)
            remote(
                borrowed, borrowed, lend_ss.at[which, 0], lend_rs.at[which], above
            ).wait_recv()

    chunks = rows // CHUNK
    parts = rows // TILE

    def chunk_rows(chunk):
        return pl.ds(pl.multiple_of(chunk * CHUNK, CHUNK), CHUNK)

    def stream_copy(part):
        at = pl.ds(part * TILE, TILE)
        return remote(
            stream.at[at, :], x.at[at, :], x_ss.at[part], x_rs.at[part], partner
        )

    out_swap = remote(
        g_out.at[:, mine_columns], g_out.at[:, mine_columns], swap_s.at[0], swap_s.at[1], beside
    )

    @pl.when(second)
    def _():
        pl.semaphore_wait(go_sem, 1)

    send_own(0)

    @pl.when(first)
    def _():
        @pl.loop(0, width // TILE)
        def _(tile):
            columns = pl.ds(pl.multiple_of(tile * TILE, TILE), TILE)
            outgoing[:, columns] = jnp.dot(
                select[...], tok[:, columns], preferred_element_type=F32
            ).astype(BF)

        for step in range(1, groups):
            token_copy(step).start()
        own_tokens.start()

    send_own(1)
    for back in range(1, half):
        relay(0, back)
    send_own(2)
    for back in range(1, half):
        relay(1, back)
        if back == 1:
            lend(1)
    send_own(3)

    @pl.when(first)
    def _():
        for step in range(1, groups):
            token_arrival(step).wait_recv()
        own_tokens.wait()

        @pl.loop(0, width // TILE)
        def _(tile):
            columns = pl.ds(pl.multiple_of(tile * TILE, TILE), TILE)
            x[:, columns] = jnp.dot(
                pick[...], received[:, columns], preferred_element_type=F32
            ).astype(BF)

    relay(2, 1)
    lend(2)
    gathered(0)
    gathered(1)
    out_swap.start()
    for back in range(2, half):
        relay(2, back)

    @pl.when(second)
    def _():
        for part in range(parts):
            stream_copy(part).wait_recv()

    @pl.loop(0, chunks)
    def _(chunk):
        at = chunk_rows(chunk)
        normed[at, :] = normalised(x[at, :].astype(F32), gain_attn[...].astype(F32)).astype(BF)

    @pl.loop(0, merged.shape[1] // TILE)
    def _(tile):
        columns = pl.ds(pl.multiple_of(tile * TILE, TILE), TILE)
        merged[:, columns] = jnp.dot(normed[...], g_qkv[:, columns], preferred_element_type=F32)

    turns = -(-(half - 1) // chunks)
    lanes = 2 * HEAD_DIM
    lane_of = lax.broadcasted_iota(jnp.int32, (CHUNK, lanes), 1)
    contract = (((1,), (1,)), ((), ()))

    def head_copy(chunk):
        at = chunk_rows(chunk)
        return remote(
            ho_mine.at[at, :], ho_other.at[at, :], ho_ss.at[chunk], ho_rs.at[chunk], beside
        )

    @pl.loop(0, chunks)
    def _(chunk):
        at = chunk_rows(chunk)
        hidden_keys = mask[chunk]
        for two in range(quarter // lanes):
            q = merged[at, two * lanes : (two + 1) * lanes]
            k = merged[at, quarter + two * lanes : quarter + (two + 1) * lanes]
            v = merged[at, 2 * quarter + two * lanes : 2 * quarter + (two + 1) * lanes].astype(BF)
            k_top = k.astype(BF)
            k_rest = (k - k_top.astype(F32)).astype(BF)
            outs = []
            for head in range(2):
                mine = (lane_of < HEAD_DIM) if head == 0 else (lane_of >= HEAD_DIM)
                q_head = jnp.where(mine, q, 0.0)
                q_top = q_head.astype(BF)
                q_rest = (q_head - q_top.astype(F32)).astype(BF)
                scores = (
                    lax.dot_general(q_top, k_top, contract, preferred_element_type=F32)
                    + lax.dot_general(q_top, k_rest, contract, preferred_element_type=F32)
                    + lax.dot_general(q_rest, k_top, contract, preferred_element_type=F32)
                ) * HEAD_DIM ** (-0.5)
                scores = scores + hidden_keys
                scores = scores - jnp.max(scores, axis=-1, keepdims=True)
                powers = jnp.exp(scores)
                total = jnp.sum(powers, axis=-1, keepdims=True)
                mixed = jnp.dot(powers.astype(BF), v, preferred_element_type=F32)
                outs.append(mixed / total)
            ho_mine[at, two * lanes : (two + 1) * lanes] = jnp.where(
                lane_of < HEAD_DIM, outs[0], outs[1]
            ).astype(BF)
        head_copy(chunk).start()
        for turn in range(turns):
            relay(3, chunk * turns + turn + 1)

    @pl.when(first)
    def _():
        pl.semaphore_signal(
            go_sem, inc=1, device_id=partner, device_id_type=pl.DeviceIdType.MESH
        )

    @pl.loop(0, chunks)
    def _(chunk):
        head_copy(chunk).wait()

    out_arrival = g_out.at[:, pl.ds(pl.multiple_of((1 - tensor) * quarter, quarter), quarter)]
    remote(out_arrival, out_arrival, swap_s.at[0], swap_s.at[1], beside).wait_recv()
    mine_rows = pl.ds(pl.multiple_of(tensor * quarter, quarter), quarter)
    other_rows = pl.ds(pl.multiple_of((1 - tensor) * quarter, quarter), quarter)

    @pl.loop(0, width // TILE)
    def _(tile):
        columns = pl.ds(pl.multiple_of(tile * TILE, TILE), TILE)
        mid[:, columns] = (
            x[:, columns].astype(F32)
            + jnp.dot(ho_mine[...], g_out[mine_rows, columns], preferred_element_type=F32)
            + jnp.dot(ho_other[...], g_out[other_rows, columns], preferred_element_type=F32)
        )

    @pl.loop(0, chunks)
    def _(chunk):
        at = chunk_rows(chunk)
        normed[at, :] = normalised(mid[at, :], gain_mlp[...].astype(F32)).astype(BF)

    gathered(2)

    @pl.loop(0, hidden.shape[1] // TILE)
    def _(tile):
        columns = pl.ds(pl.multiple_of(tile * TILE, TILE), TILE)
        raised = (
            jnp.dot(normed[...], g_up[:, columns], preferred_element_type=F32)
            + bias[:, columns].astype(F32)
        )
        hidden[:, columns] = (raised * (1.0 + lax.erf(raised * (0.5**0.5))) * 0.5).astype(BF)

    def partial_copy(part):
        at = pl.ds(part * TILE, TILE)
        return remote(p_mine.at[at, :], p_other.at[at, :], p_ss.at[part], p_rs.at[part], beside)

    gathered(3)

    for part in range(parts):
        at = pl.ds(part * TILE, TILE)

        @pl.loop(0, width // TILE)
        def _(tile):
            columns = pl.ds(pl.multiple_of(tile * TILE, TILE), TILE)
            if narrow:
                count = TILE // g_down.shape[2]
                product = jnp.concatenate(
                    [
                        jnp.dot(
                            hidden[at, :], g_down[tile * count + i], preferred_element_type=F32
                        )
                        for i in range(count)
                    ],
                    axis=1,
                )
            else:
                product = jnp.dot(hidden[at, :], g_down[:, columns], preferred_element_type=F32)
            p_mine[at, columns] = product.astype(BF)

        partial_copy(part).start()

    for part in range(parts):
        at = pl.ds(part * TILE, TILE)
        partial_copy(part).wait()
        stream[at, :] = (
            mid[at, :] + (p_mine[at, :].astype(F32) + p_other[at, :].astype(F32))
        ).astype(BF)

        @pl.when(first)
        def _():
            stream_copy(part).start()

    result = remote(
        fin.at[:, pl.ds(0, section_rows), :], o_ref, fin_s.at[0], fin_s.at[1], partner
    )

    @pl.when(second)
    def _():
        per = CHUNK // block
        own_columns = pl.ds(pl.multiple_of(tensor * quarter, quarter), quarter)

        @pl.loop(0, chunks)
        def _(chunk):
            at = chunk_rows(chunk)
            values = stream[at, :].astype(F32)
            average = jnp.mean(values, axis=-1, keepdims=True)
            centred = values - average
            scale = lax.rsqrt(jnp.mean(centred * centred, axis=-1, keepdims=True) + epsilon)
            piece_values = (
                (stream[at, own_columns].astype(F32) - average) * scale * gain_final[:, own_columns].astype(F32)
            )
            fin[pl.ds(chunk * per, per)] = piece_values.astype(BF).reshape(per, block, quarter)

        result.start()
        o_ref[...] = fin[:, section_rows:, :]
        result.wait_send()

    @pl.when(first)
    def _():
        for part in range(parts):
            stream_copy(part).wait_send()
        for step in range(1, groups):
            token_copy(step).wait_send()
        result.wait_recv()

    out_swap.wait_send()
    for which in range(4):
        source = sources[which]
        for back in range(half):

            @pl.when(has_above & (high - back >= 0))
            def _():
                up_copy(which, high - back, source).wait_send()

            @pl.when(has_below & (high + back < half))
            def _():
                down_copy(which, high + back, source).wait_send()

            if which in lent:

                @pl.when(lender != back)
                def _():
                    pair_copy(which, back, source).wait_send()

            else:
                pair_copy(which, back, source).wait_send()
        if which in lent:

            @pl.when(lends_below)
            def _():
                lend_copy(which, 0).wait_send()

            @pl.when(lends_above)
            def _():
                lend_copy(which, 1).wait_send()


def local(
    tokens,
    counts,
    assign,
    qkv_weight,
    out_weight,
    up_weight,
    up_bias,
    down_weight,
    attn_gain,
    mlp_gain,
    final_gain,
):
    groups = lax.axis_size("dp")
    sections = lax.axis_size("section")
    tensor_ranks = lax.axis_size("tensor")
    images_dev, block, width = tokens.shape
    quarter = width // tensor_ranks
    capacity = (images_dev + groups - 1) // groups
    total_images = assign.shape[0]
    rows = images_dev * block
    slots = groups * capacity
    my_group = lax.axis_index("dp")
    numbers = jnp.arange(total_images, dtype=jnp.int32)
    matches = (assign[:, None] == numbers[None, :]).astype(jnp.int32)
    slot_of = jnp.sum(matches * numbers[:, None], axis=0)
    target = slot_of // images_dev
    source_group = numbers // images_dev
    earlier = (
        (source_group[:, None] == source_group[None, :])
        & (target[:, None] == target[None, :])
        & (numbers[None, :] < numbers[:, None])
    )
    rank_all = jnp.sum(earlier.astype(jnp.int32), axis=1)
    send_slot = lax.dynamic_slice_in_dim(
        target * capacity + rank_all, my_group * images_dev, images_dev
    )
    my_images = lax.dynamic_slice_in_dim(assign, my_group * images_dev, images_dev)
    chosen = (my_images[:, None] == numbers[None, :]).astype(jnp.int32)
    receive_slot = jnp.sum(chosen * (source_group * capacity + rank_all)[None, :], axis=1)
    live_counts = jnp.sum(chosen * counts[None, :], axis=1)
    within = jnp.tile(jnp.arange(block, dtype=jnp.int32), images_dev)
    buffer_rows = jnp.arange(slots * block, dtype=jnp.int32)
    send_rows = jnp.repeat(send_slot, block) * block + within
    receive_rows = jnp.repeat(receive_slot, block) * block + within
    select = (buffer_rows[:, None] == send_rows[None, :]).astype(BF)
    pick = (buffer_rows[None, :] == receive_rows[:, None]).astype(BF)
    per = CHUNK // block
    key_live = within.reshape(-1, CHUNK) < jnp.repeat(live_counts, block).reshape(-1, CHUNK)
    image_of = jnp.arange(CHUNK) // block
    visible = key_live[:, None, :] & (image_of[:, None] == image_of[None, :])[None]
    mask = jnp.where(visible, 0.0, -1e30).astype(F32)
    w_qkv = qkv_weight[0].reshape(qkv_weight.shape[1], -1)
    w_out, w_up, w_down = out_weight[0], up_weight[0], down_weight[0]
    units = w_up.shape[1]
    down_columns = w_down.shape[1]
    down_shape = (units, width) if down_columns % 128 == 0 else (groups, units, down_columns)
    half = groups // 2
    cap_rows = capacity * block
    vmem = pl.BlockSpec(memory_space=pltpu.VMEM)
    anywhere = pl.BlockSpec(memory_space=pl.ANY)
    dma = pltpu.SemaphoreType.DMA
    section_rows = block // sections
    encoded = pl.pallas_call(
        functools.partial(encoder, groups, cap_rows),
        out_shape=jax.ShapeDtypeStruct((images_dev, section_rows, quarter), BF),
        in_specs=[vmem] * 8 + [anywhere] * 4,
        out_specs=vmem,
        scratch_shapes=[
            pltpu.VMEM((width, w_qkv.shape[1]), BF),
            pltpu.VMEM((width, width), BF),
            pltpu.VMEM((width, units), BF),
            pltpu.VMEM(down_shape, BF),
            pltpu.VMEM((slots * block, width), BF),
            pltpu.VMEM((slots * block, width), BF),
            pltpu.VMEM((rows, width), BF),
            pltpu.VMEM((rows, width), BF),
            pltpu.VMEM((rows, w_qkv.shape[1]), F32),
            pltpu.VMEM((rows, quarter), BF),
            pltpu.VMEM((rows, quarter), BF),
            pltpu.VMEM((rows, width), F32),
            pltpu.VMEM((rows, units), BF),
            pltpu.VMEM((rows, width), BF),
            pltpu.VMEM((rows, width), BF),
            pltpu.VMEM((rows, width), BF),
            pltpu.VMEM((images_dev, block, quarter), BF),
            dma((groups,)),
            dma((groups,)),
            dma((4,)),
            dma((4, half)),
            dma((4, half)),
            dma((4, half)),
            dma((4, half)),
            dma((4, half)),
            dma((rows // CHUNK,)),
            dma((rows // CHUNK,)),
            dma((rows // TILE,)),
            dma((rows // TILE,)),
            dma((rows // TILE,)),
            dma((rows // TILE,)),
            dma((2,)),
            dma((4, 2)),
            dma((4,)),
            dma((2,)),
            pltpu.SemaphoreType.REGULAR,
        ],
        compiler_params=pltpu.CompilerParams(
            collective_id=0, has_side_effects=True, vmem_limit_bytes=60 * 1024 * 1024
        ),
    )(
        tokens.reshape(rows, width),
        select,
        pick,
        mask,
        up_bias,
        attn_gain,
        mlp_gain,
        final_gain[None],
        w_qkv,
        w_out,
        w_up,
        w_down,
    )
    row_numbers = lax.axis_index("section") * section_rows + jnp.arange(section_rows)
    alive = row_numbers[None, :, None] < live_counts[:, None, None]
    return jnp.where(alive, encoded, jnp.zeros_like(encoded))


def solution(mesh):
    in_specs = (
        P("dp", None, None),
        P(),
        P(),
        P("section", "dp", None, "tensor"),
        P("section", "dp", None),
        P("section", "dp", "tensor"),
        P("section", "tensor"),
        P("section", "tensor", "dp"),
        P("section", None),
        P("section", None),
        P(),
    )
    out_specs = P("dp", "section", "tensor")
    return jax.shard_map(local, mesh=mesh, in_specs=in_specs, out_specs=out_specs, check_vma=False)
```

```python
import functools

import jax
import jax.numpy as jnp
from jax import lax
from jax.experimental import pallas as pl
from jax.experimental.pallas import tpu as pltpu
from jax.sharding import PartitionSpec as P

HEAD_DIM = 64
CHUNK = 128
TILE = 256
epsilon = 1e-06
BF = jnp.bfloat16
F32 = jnp.float32


def normalised(values, gain_row):
    average = jnp.mean(values, axis=-1, keepdims=True)
    centred = values - average
    spread = jnp.mean(centred * centred, axis=-1, keepdims=True)
    return centred * lax.rsqrt(spread + epsilon) * gain_row


def encoder(
    groups,
    cap_rows,
    tok,
    select,
    pick,
    mask,
    bias,
    gain_attn,
    gain_mlp,
    gain_final,
    w_qkv,
    w_out,
    w_up,
    w_down,
    o_ref,
    g_qkv,
    g_out,
    g_up,
    g_down,
    outgoing,
    received,
    x,
    normed,
    merged,
    ho_mine,
    ho_other,
    mid,
    hidden,
    p_mine,
    p_other,
    stream,
    fin,
    tok_ss,
    tok_rs,
    own_s,
    line_up,
    line_down,
    line_rs,
    pair_ss,
    pair_rs,
    ho_ss,
    ho_rs,
    p_ss,
    p_rs,
    x_ss,
    x_rs,
    fin_s,
    lend_ss,
    lend_rs,
    swap_s,
    go_sem,
):
    me = lax.axis_index("dp")
    section = lax.axis_index("section")
    tensor = lax.axis_index("tensor")
    half = groups // 2
    high, low = me // 2, me % 2
    rows, width = tok.shape
    quarter = ho_mine.shape[1]
    images, section_rows, _ = o_ref.shape
    block = fin.shape[1]
    above = {"dp": jnp.minimum(high + 1, half - 1) * 2 + low}
    below = {"dp": jnp.maximum(high - 1, 0) * 2 + low}
    pair = {"dp": high * 2 + 1 - low}
    beside = {"tensor": 1 - tensor}
    partner = {"section": 1 - section}

    def remote(src, dst, ss, rs, device):
        return pltpu.make_async_remote_copy(
            src_ref=src,
            dst_ref=dst,
            send_sem=ss,
            recv_sem=rs,
            device_id=device,
            device_id_type=pl.DeviceIdType.MESH,
        )

    barrier = pltpu.get_barrier_semaphore()
    for step in range(1, groups):
        pl.semaphore_signal(
            barrier,
            inc=1,
            device_id={"dp": (me + step) % groups},
            device_id_type=pl.DeviceIdType.MESH,
        )
    for device in (beside, partner):
        pl.semaphore_signal(
            barrier, inc=1, device_id=device, device_id_type=pl.DeviceIdType.MESH
        )
    pl.semaphore_wait(barrier, groups + 1)

    narrow = len(g_down.shape) == 3
    mine_columns = pl.ds(pl.multiple_of(tensor * quarter, quarter), quarter)
    sources = (w_qkv, w_out.at[:, mine_columns], w_up, w_down)
    wholes = (g_qkv, g_out, g_up, g_down)
    lent = (0, 1)

    def piece(which, number):
        source, whole = sources[which], wholes[which]
        if which < 3:
            size = source.shape[0]
            at = pl.ds(pl.multiple_of(number * size, size), size)
            return whole.at[at, mine_columns] if which == 1 else whole.at[at, :]
        if narrow:
            return whole.at[number]
        size = source.shape[1]
        return whole.at[:, pl.ds(pl.multiple_of(number * size, size), size)]

    def slot(buffer, number):
        return buffer.at[pl.ds(pl.multiple_of(number * cap_rows, cap_rows), cap_rows), :]

    first = section == 0
    second = section == 1

    def token_copy(step):
        peer = (me + step) % groups
        return remote(
            slot(outgoing, peer), slot(received, me), tok_ss.at[peer], tok_rs.at[me], {"dp": peer}
        )

    def token_arrival(step):
        peer = (me + step) % groups
        return remote(
            slot(outgoing, peer), slot(received, peer), tok_ss.at[peer], tok_rs.at[peer], {"dp": peer}
        )

    own_tokens = pltpu.make_async_copy(slot(outgoing, me), slot(received, me), tok_ss.at[me])

    def up_copy(which, source_high, src):
        return remote(
            src,
            piece(which, source_high * 2 + low),
            line_up.at[which, source_high],
            line_rs.at[which, source_high],
            above,
        )

    def down_copy(which, source_high, src):
        return remote(
            src,
            piece(which, source_high * 2 + low),
            line_down.at[which, source_high],
            line_rs.at[which, source_high],
            below,
        )

    def pair_copy(which, source_high, src):
        return remote(
            src,
            piece(which, source_high * 2 + low),
            pair_ss.at[which, source_high],
            pair_rs.at[which, source_high],
            pair,
        )

    has_above = high < half - 1
    has_below = high > 0
    in_lower = high < half // 2
    lends_above = has_above & (high + 1 >= half // 2)
    lends_below = has_below & (high - 1 < half // 2)
    lender = jnp.where(in_lower, high + 1, high - 1)

    owns = [
        pltpu.make_async_copy(sources[which], piece(which, me), own_s.at[which])
        for which in range(4)
    ]

    def send_own(which):
        source = sources[which]

        @pl.when(has_above)
        def _():
            up_copy(which, high, source).start()

        @pl.when(has_below)
        def _():
            down_copy(which, high, source).start()

        pair_copy(which, high, source).start()
        owns[which].start()

    def relay(which, back):
        lower = high - back

        @pl.when(lower >= 0)
        def _():
            src = piece(which, lower * 2 + low)
            up_copy(which, lower, src).wait_recv()

            @pl.when(has_above)
            def _():
                up_copy(which, lower, src).start()

            if which in lent:

                @pl.when(lower != lender)
                def _():
                    pair_copy(which, lower, src).start()

            else:
                pair_copy(which, lower, src).start()

        upper = high + back

        @pl.when(upper < half)
        def _():
            src = piece(which, upper * 2 + low)
            down_copy(which, upper, src).wait_recv()

            @pl.when(has_below)
            def _():
                down_copy(which, upper, src).start()

            if which in lent:

                @pl.when(upper != lender)
                def _():
                    pair_copy(which, upper, src).start()

            else:
                pair_copy(which, upper, src).start()

    def pair_arrival(which, source_high):
        other = piece(which, source_high * 2 + 1 - low)
        return remote(
            other, other, pair_ss.at[which, source_high], pair_rs.at[which, source_high], pair
        )

    def lend_copy(which, direction):
        other = piece(which, high * 2 + 1 - low)
        return remote(
            other,
            other,
            lend_ss.at[which, direction],
            lend_rs.at[which],
            below if direction == 0 else above,
        )

    def lend(which):
        pair_arrival(which, high).wait_recv()

        @pl.when(lends_below)
        def _():
            lend_copy(which, 0).start()

        @pl.when(lends_above)
        def _():
            lend_copy(which, 1).start()

    def gathered(which):
        owns[which].wait()
        for source_high in range(half):
            if which in lent:

                @pl.when((high != source_high) & (lender != source_high))
                def _():
                    pair_arrival(which, source_high).wait_recv()

            else:
                pair_arrival(which, source_high).wait_recv()
        if which in lent:
            borrowed = piece(which, lender * 2 + 1 - low)
            remote(
                borrowed, borrowed, lend_ss.at[which, 0], lend_rs.at[which], above
            ).wait_recv()

    chunks = rows // CHUNK
    parts = rows // TILE

    def chunk_rows(chunk):
        return pl.ds(pl.multiple_of(chunk * CHUNK, CHUNK), CHUNK)

    def stream_copy(part):
        at = pl.ds(part * TILE, TILE)
        return remote(
            stream.at[at, :], x.at[at, :], x_ss.at[part], x_rs.at[part], partner
        )

    out_swap = remote(
        g_out.at[:, mine_columns], g_out.at[:, mine_columns], swap_s.at[0], swap_s.at[1], beside
    )

    @pl.when(second)
    def _():
        pl.semaphore_wait(go_sem, 1)

    send_own(0)

    @pl.when(first)
    def _():
        @pl.loop(0, width // TILE)
        def _(tile):
            columns = pl.ds(pl.multiple_of(tile * TILE, TILE), TILE)
            outgoing[:, columns] = jnp.dot(
                select[...], tok[:, columns], preferred_element_type=F32
            ).astype(BF)

        for step in range(1, groups):
            token_copy(step).start()
        own_tokens.start()

    send_own(1)
    for back in range(1, half):
        relay(0, back)
        if back == 1 and 0 in lent:
            lend(0)
    send_own(2)
    for back in range(1, half):
        relay(1, back)
        if back == 1 and 1 in lent:
            lend(1)
    send_own(3)

    @pl.when(first)
    def _():
        for step in range(1, groups):
            token_arrival(step).wait_recv()
        own_tokens.wait()

        @pl.loop(0, width // TILE)
        def _(tile):
            columns = pl.ds(pl.multiple_of(tile * TILE, TILE), TILE)
            x[:, columns] = jnp.dot(
                pick[...], received[:, columns], preferred_element_type=F32
            ).astype(BF)

    relay(2, 1)
    if 2 in lent:
        lend(2)
    gathered(0)
    gathered(1)
    out_swap.start()
    for back in range(2, half):
        relay(2, back)

    @pl.when(second)
    def _():
        for part in range(parts):
            stream_copy(part).wait_recv()

    @pl.loop(0, chunks)
    def _(chunk):
        at = chunk_rows(chunk)
        normed[at, :] = normalised(x[at, :].astype(F32), gain_attn[...].astype(F32)).astype(BF)

    @pl.loop(0, merged.shape[1] // TILE)
    def _(tile):
        columns = pl.ds(pl.multiple_of(tile * TILE, TILE), TILE)
        merged[:, columns] = jnp.dot(normed[...], g_qkv[:, columns], preferred_element_type=F32)

    turns = -(-(half - 1) // chunks)
    lanes = 2 * HEAD_DIM
    lane_of = lax.broadcasted_iota(jnp.int32, (CHUNK, lanes), 1)
    contract = (((1,), (1,)), ((), ()))

    def head_copy(chunk):
        at = chunk_rows(chunk)
        return remote(
            ho_mine.at[at, :], ho_other.at[at, :], ho_ss.at[chunk], ho_rs.at[chunk], beside
        )

    @pl.loop(0, chunks)
    def _(chunk):
        at = chunk_rows(chunk)
        hidden_keys = mask[chunk]
        for two in range(quarter // lanes):
            q = merged[at, two * lanes : (two + 1) * lanes]
            k = merged[at, quarter + two * lanes : quarter + (two + 1) * lanes]
            v = merged[at, 2 * quarter + two * lanes : 2 * quarter + (two + 1) * lanes].astype(BF)
            k_top = k.astype(BF)
            k_rest = (k - k_top.astype(F32)).astype(BF)
            outs = []
            for head in range(2):
                mine = (lane_of < HEAD_DIM) if head == 0 else (lane_of >= HEAD_DIM)
                q_head = jnp.where(mine, q, 0.0)
                q_top = q_head.astype(BF)
                q_rest = (q_head - q_top.astype(F32)).astype(BF)
                scores = (
                    lax.dot_general(q_top, k_top, contract, preferred_element_type=F32)
                    + lax.dot_general(q_top, k_rest, contract, preferred_element_type=F32)
                    + lax.dot_general(q_rest, k_top, contract, preferred_element_type=F32)
                ) * HEAD_DIM ** (-0.5)
                scores = scores + hidden_keys
                scores = scores - jnp.max(scores, axis=-1, keepdims=True)
                powers = jnp.exp(scores)
                total = jnp.sum(powers, axis=-1, keepdims=True)
                mixed = jnp.dot(powers.astype(BF), v, preferred_element_type=F32)
                outs.append(mixed / total)
            ho_mine[at, two * lanes : (two + 1) * lanes] = jnp.where(
                lane_of < HEAD_DIM, outs[0], outs[1]
            ).astype(BF)
        head_copy(chunk).start()
        for turn in range(turns):
            relay(3, chunk * turns + turn + 1)

    @pl.when(first)
    def _():
        pl.semaphore_signal(
            go_sem, inc=1, device_id=partner, device_id_type=pl.DeviceIdType.MESH
        )

    @pl.loop(0, chunks)
    def _(chunk):
        head_copy(chunk).wait()

    out_arrival = g_out.at[:, pl.ds(pl.multiple_of((1 - tensor) * quarter, quarter), quarter)]
    remote(out_arrival, out_arrival, swap_s.at[0], swap_s.at[1], beside).wait_recv()
    mine_rows = pl.ds(pl.multiple_of(tensor * quarter, quarter), quarter)
    other_rows = pl.ds(pl.multiple_of((1 - tensor) * quarter, quarter), quarter)

    @pl.loop(0, width // TILE)
    def _(tile):
        columns = pl.ds(pl.multiple_of(tile * TILE, TILE), TILE)
        mid[:, columns] = (
            x[:, columns].astype(F32)
            + jnp.dot(ho_mine[...], g_out[mine_rows, columns], preferred_element_type=F32)
            + jnp.dot(ho_other[...], g_out[other_rows, columns], preferred_element_type=F32)
        )

    @pl.loop(0, chunks)
    def _(chunk):
        at = chunk_rows(chunk)
        normed[at, :] = normalised(mid[at, :], gain_mlp[...].astype(F32)).astype(BF)

    gathered(2)

    @pl.loop(0, hidden.shape[1] // TILE)
    def _(tile):
        columns = pl.ds(pl.multiple_of(tile * TILE, TILE), TILE)
        raised = (
            jnp.dot(normed[...], g_up[:, columns], preferred_element_type=F32)
            + bias[:, columns].astype(F32)
        )
        hidden[:, columns] = (raised * (1.0 + lax.erf(raised * (0.5**0.5))) * 0.5).astype(BF)

    size_down = w_down.shape[1]

    def partial_copy(number):
        return remote(
            p_mine.at[number], p_other.at[number], p_ss.at[number], p_rs.at[number], beside
        )

    def partial(number):
        if narrow:
            columns_of = g_down[number]
        else:
            columns_of = g_down[:, pl.ds(pl.multiple_of(number * size_down, size_down), size_down)]
        p_mine[number] = jnp.dot(hidden[...], columns_of, preferred_element_type=F32).astype(BF)
        partial_copy(number).start()

    owns[3].wait()

    @pl.loop(0, half)
    def _(source_high):
        partial(source_high * 2 + low)

    @pl.loop(0, half)
    def _(step):
        source_high = jnp.where(in_lower, high + step, high - step + half) % half
        pair_arrival(3, source_high).wait_recv()
        partial(source_high * 2 + 1 - low)

    if narrow:
        joined = TILE // size_down
        tiles = [
            (slice(t * TILE, (t + 1) * TILE), [t * joined + i for i in range(joined)])
            for t in range(width // TILE)
        ]
    else:
        tiles = [
            (slice(t * size_down, (t + 1) * size_down), [t]) for t in range(width // size_down)
        ]
    for number in range(groups):
        partial_copy(number).wait()

    @pl.loop(0, parts)
    def _(part):
        at = pl.ds(pl.multiple_of(part * TILE, TILE), TILE)
        for columns, numbers in tiles:
            added = [
                p_mine[number, at, :].astype(F32) + p_other[number, at, :].astype(F32)
                for number in numbers
            ]
            added = added[0] if len(added) == 1 else jnp.concatenate(added, axis=1)
            stream[at, columns] = (mid[at, columns] + added).astype(BF)

    @pl.when(first)
    def _():
        for part in range(parts):
            stream_copy(part).start()

    result = remote(
        fin.at[:, pl.ds(0, section_rows), :], o_ref, fin_s.at[0], fin_s.at[1], partner
    )

    @pl.when(second)
    def _():
        per = CHUNK // block
        own_columns = pl.ds(pl.multiple_of(tensor * quarter, quarter), quarter)

        @pl.loop(0, chunks)
        def _(chunk):
            at = chunk_rows(chunk)
            values = stream[at, :].astype(F32)
            average = jnp.mean(values, axis=-1, keepdims=True)
            centred = values - average
            scale = lax.rsqrt(jnp.mean(centred * centred, axis=-1, keepdims=True) + epsilon)
            piece_values = (
                (stream[at, own_columns].astype(F32) - average) * scale * gain_final[:, own_columns].astype(F32)
            )
            fin[pl.ds(chunk * per, per)] = piece_values.astype(BF).reshape(per, block, quarter)

        result.start()
        o_ref[...] = fin[:, section_rows:, :]
        result.wait_send()

    @pl.when(first)
    def _():
        for part in range(parts):
            stream_copy(part).wait_send()
        for step in range(1, groups):
            token_copy(step).wait_send()
        result.wait_recv()

    out_swap.wait_send()
    for which in range(4):
        source = sources[which]
        for back in range(half):

            @pl.when(has_above & (high - back >= 0))
            def _():
                up_copy(which, high - back, source).wait_send()

            @pl.when(has_below & (high + back < half))
            def _():
                down_copy(which, high + back, source).wait_send()

            if which in lent:

                @pl.when(lender != back)
                def _():
                    pair_copy(which, back, source).wait_send()

            else:
                pair_copy(which, back, source).wait_send()
        if which in lent:

            @pl.when(lends_below)
            def _():
                lend_copy(which, 0).wait_send()

            @pl.when(lends_above)
            def _():
                lend_copy(which, 1).wait_send()


def local(
    tokens,
    counts,
    assign,
    qkv_weight,
    out_weight,
    up_weight,
    up_bias,
    down_weight,
    attn_gain,
    mlp_gain,
    final_gain,
):
    groups = lax.axis_size("dp")
    sections = lax.axis_size("section")
    tensor_ranks = lax.axis_size("tensor")
    images_dev, block, width = tokens.shape
    quarter = width // tensor_ranks
    capacity = (images_dev + groups - 1) // groups
    total_images = assign.shape[0]
    rows = images_dev * block
    slots = groups * capacity
    my_group = lax.axis_index("dp")
    numbers = jnp.arange(total_images, dtype=jnp.int32)
    matches = (assign[:, None] == numbers[None, :]).astype(jnp.int32)
    slot_of = jnp.sum(matches * numbers[:, None], axis=0)
    target = slot_of // images_dev
    source_group = numbers // images_dev
    earlier = (
        (source_group[:, None] == source_group[None, :])
        & (target[:, None] == target[None, :])
        & (numbers[None, :] < numbers[:, None])
    )
    rank_all = jnp.sum(earlier.astype(jnp.int32), axis=1)
    send_slot = lax.dynamic_slice_in_dim(
        target * capacity + rank_all, my_group * images_dev, images_dev
    )
    my_images = lax.dynamic_slice_in_dim(assign, my_group * images_dev, images_dev)
    chosen = (my_images[:, None] == numbers[None, :]).astype(jnp.int32)
    receive_slot = jnp.sum(chosen * (source_group * capacity + rank_all)[None, :], axis=1)
    live_counts = jnp.sum(chosen * counts[None, :], axis=1)
    within = jnp.tile(jnp.arange(block, dtype=jnp.int32), images_dev)
    buffer_rows = jnp.arange(slots * block, dtype=jnp.int32)
    send_rows = jnp.repeat(send_slot, block) * block + within
    receive_rows = jnp.repeat(receive_slot, block) * block + within
    select = (buffer_rows[:, None] == send_rows[None, :]).astype(BF)
    pick = (buffer_rows[None, :] == receive_rows[:, None]).astype(BF)
    per = CHUNK // block
    key_live = within.reshape(-1, CHUNK) < jnp.repeat(live_counts, block).reshape(-1, CHUNK)
    image_of = jnp.arange(CHUNK) // block
    visible = key_live[:, None, :] & (image_of[:, None] == image_of[None, :])[None]
    mask = jnp.where(visible, 0.0, -1e30).astype(F32)
    w_qkv = qkv_weight[0].reshape(qkv_weight.shape[1], -1)
    w_out, w_up, w_down = out_weight[0], up_weight[0], down_weight[0]
    units = w_up.shape[1]
    down_columns = w_down.shape[1]
    down_shape = (units, width) if down_columns % 128 == 0 else (groups, units, down_columns)
    half = groups // 2
    cap_rows = capacity * block
    vmem = pl.BlockSpec(memory_space=pltpu.VMEM)
    anywhere = pl.BlockSpec(memory_space=pl.ANY)
    dma = pltpu.SemaphoreType.DMA
    section_rows = block // sections
    encoded = pl.pallas_call(
        functools.partial(encoder, groups, cap_rows),
        out_shape=jax.ShapeDtypeStruct((images_dev, section_rows, quarter), BF),
        in_specs=[vmem] * 8 + [anywhere] * 4,
        out_specs=vmem,
        scratch_shapes=[
            pltpu.VMEM((width, w_qkv.shape[1]), BF),
            pltpu.VMEM((width, width), BF),
            pltpu.VMEM((width, units), BF),
            pltpu.VMEM(down_shape, BF),
            pltpu.VMEM((slots * block, width), BF),
            pltpu.VMEM((slots * block, width), BF),
            pltpu.VMEM((rows, width), BF),
            pltpu.VMEM((rows, width), BF),
            pltpu.VMEM((rows, w_qkv.shape[1]), F32),
            pltpu.VMEM((rows, quarter), BF),
            pltpu.VMEM((rows, quarter), BF),
            pltpu.VMEM((rows, width), F32),
            pltpu.VMEM((rows, units), BF),
            pltpu.VMEM((groups, rows, down_columns), BF),
            pltpu.VMEM((groups, rows, down_columns), BF),
            pltpu.VMEM((rows, width), BF),
            pltpu.VMEM((images_dev, block, quarter), BF),
            dma((groups,)),
            dma((groups,)),
            dma((4,)),
            dma((4, half)),
            dma((4, half)),
            dma((4, half)),
            dma((4, half)),
            dma((4, half)),
            dma((rows // CHUNK,)),
            dma((rows // CHUNK,)),
            dma((groups,)),
            dma((groups,)),
            dma((rows // TILE,)),
            dma((rows // TILE,)),
            dma((2,)),
            dma((4, 2)),
            dma((4,)),
            dma((2,)),
            pltpu.SemaphoreType.REGULAR,
        ],
        compiler_params=pltpu.CompilerParams(
            collective_id=0, has_side_effects=True, vmem_limit_bytes=60 * 1024 * 1024
        ),
    )(
        tokens.reshape(rows, width),
        select,
        pick,
        mask,
        up_bias,
        attn_gain,
        mlp_gain,
        final_gain[None],
        w_qkv,
        w_out,
        w_up,
        w_down,
    )
    row_numbers = lax.axis_index("section") * section_rows + jnp.arange(section_rows)
    alive = row_numbers[None, :, None] < live_counts[:, None, None]
    return jnp.where(alive, encoded, jnp.zeros_like(encoded))


def solution(mesh):
    in_specs = (
        P("dp", None, None),
        P(),
        P(),
        P("section", "dp", None, "tensor"),
        P("section", "dp", None),
        P("section", "dp", "tensor"),
        P("section", "tensor"),
        P("section", "tensor", "dp"),
        P("section", None),
        P("section", None),
        P(),
    )
    out_specs = P("dp", "section", "tensor")
    return jax.shard_map(local, mesh=mesh, in_specs=in_specs, out_specs=out_specs, check_vma=False)
```

```python
import functools

import jax
import jax.numpy as jnp
from jax import lax
from jax.experimental import pallas as pl
from jax.experimental.pallas import tpu as pltpu
from jax.sharding import PartitionSpec as P

HEAD_DIM = 64
CHUNK = 128
TILE = 256
epsilon = 1e-06
BF = jnp.bfloat16
F32 = jnp.float32


def normalised(values, gain_row):
    average = jnp.mean(values, axis=-1, keepdims=True)
    centred = values - average
    spread = jnp.mean(centred * centred, axis=-1, keepdims=True)
    return centred * lax.rsqrt(spread + epsilon) * gain_row


def encoder(
    groups,
    cap_rows,
    tok,
    select,
    pick,
    mask,
    bias,
    gain_attn,
    gain_mlp,
    gain_final,
    w_qkv,
    w_out,
    w_up,
    w_down,
    o_ref,
    g_qkv,
    g_out,
    g_up,
    g_down,
    outgoing,
    received,
    x,
    normed,
    merged,
    ho_mine,
    ho_other,
    mid,
    hidden,
    p_mine,
    p_other,
    stream,
    fin,
    tok_ss,
    tok_rs,
    own_s,
    line_up,
    line_down,
    line_rs,
    pair_ss,
    pair_rs,
    ho_ss,
    ho_rs,
    p_ss,
    p_rs,
    x_ss,
    x_rs,
    fin_s,
    lend_ss,
    lend_rs,
    swap_s,
    go_sem,
):
    me = lax.axis_index("dp")
    section = lax.axis_index("section")
    tensor = lax.axis_index("tensor")
    half = groups // 2
    high, low = me // 2, me % 2
    rows, width = tok.shape
    quarter = ho_mine.shape[1]
    images, section_rows, _ = o_ref.shape
    block = fin.shape[1]
    above = {"dp": jnp.minimum(high + 1, half - 1) * 2 + low}
    below = {"dp": jnp.maximum(high - 1, 0) * 2 + low}
    pair = {"dp": high * 2 + 1 - low}
    beside = {"tensor": 1 - tensor}
    partner = {"section": 1 - section}

    def remote(src, dst, ss, rs, device):
        return pltpu.make_async_remote_copy(
            src_ref=src,
            dst_ref=dst,
            send_sem=ss,
            recv_sem=rs,
            device_id=device,
            device_id_type=pl.DeviceIdType.MESH,
        )

    barrier = pltpu.get_barrier_semaphore()
    for step in range(1, groups):
        pl.semaphore_signal(
            barrier,
            inc=1,
            device_id={"dp": (me + step) % groups},
            device_id_type=pl.DeviceIdType.MESH,
        )
    for device in (beside, partner):
        pl.semaphore_signal(
            barrier, inc=1, device_id=device, device_id_type=pl.DeviceIdType.MESH
        )
    pl.semaphore_wait(barrier, groups + 1)

    narrow = len(g_down.shape) == 3
    mine_columns = pl.ds(pl.multiple_of(tensor * quarter, quarter), quarter)
    sources = (w_qkv, w_out.at[:, mine_columns], w_up, w_down)
    wholes = (g_qkv, g_out, g_up, g_down)
    lent = (0, 1)

    def piece(which, number):
        source, whole = sources[which], wholes[which]
        if which < 3:
            size = source.shape[0]
            at = pl.ds(pl.multiple_of(number * size, size), size)
            return whole.at[at, mine_columns] if which == 1 else whole.at[at, :]
        if narrow:
            return whole.at[number]
        size = source.shape[1]
        return whole.at[:, pl.ds(pl.multiple_of(number * size, size), size)]

    def slot(buffer, number):
        return buffer.at[pl.ds(pl.multiple_of(number * cap_rows, cap_rows), cap_rows), :]

    first = section == 0
    second = section == 1

    def token_copy(step):
        peer = (me + step) % groups
        return remote(
            slot(outgoing, peer), slot(received, me), tok_ss.at[peer], tok_rs.at[me], {"dp": peer}
        )

    def token_arrival(step):
        peer = (me + step) % groups
        return remote(
            slot(outgoing, peer), slot(received, peer), tok_ss.at[peer], tok_rs.at[peer], {"dp": peer}
        )

    own_tokens = pltpu.make_async_copy(slot(outgoing, me), slot(received, me), tok_ss.at[me])

    def up_copy(which, source_high, src):
        return remote(
            src,
            piece(which, source_high * 2 + low),
            line_up.at[which, source_high],
            line_rs.at[which, source_high],
            above,
        )

    def down_copy(which, source_high, src):
        return remote(
            src,
            piece(which, source_high * 2 + low),
            line_down.at[which, source_high],
            line_rs.at[which, source_high],
            below,
        )

    def pair_copy(which, source_high, src):
        return remote(
            src,
            piece(which, source_high * 2 + low),
            pair_ss.at[which, source_high],
            pair_rs.at[which, source_high],
            pair,
        )

    has_above = high < half - 1
    has_below = high > 0
    in_lower = high < half // 2
    lends_above = has_above & (high + 1 >= half // 2)
    lends_below = has_below & (high - 1 < half // 2)
    lender = jnp.where(in_lower, high + 1, high - 1)

    owns = [
        pltpu.make_async_copy(sources[which], piece(which, me), own_s.at[which])
        for which in range(4)
    ]

    def send_own(which):
        source = sources[which]

        @pl.when(has_above)
        def _():
            up_copy(which, high, source).start()

        @pl.when(has_below)
        def _():
            down_copy(which, high, source).start()

        pair_copy(which, high, source).start()
        owns[which].start()

    def relay(which, back):
        lower = high - back

        @pl.when(lower >= 0)
        def _():
            src = piece(which, lower * 2 + low)
            up_copy(which, lower, src).wait_recv()

            @pl.when(has_above)
            def _():
                up_copy(which, lower, src).start()

            if which in lent:

                @pl.when(lower != lender)
                def _():
                    pair_copy(which, lower, src).start()

            else:
                pair_copy(which, lower, src).start()

        upper = high + back

        @pl.when(upper < half)
        def _():
            src = piece(which, upper * 2 + low)
            down_copy(which, upper, src).wait_recv()

            @pl.when(has_below)
            def _():
                down_copy(which, upper, src).start()

            if which in lent:

                @pl.when(upper != lender)
                def _():
                    pair_copy(which, upper, src).start()

            else:
                pair_copy(which, upper, src).start()

    def pair_arrival(which, source_high):
        other = piece(which, source_high * 2 + 1 - low)
        return remote(
            other, other, pair_ss.at[which, source_high], pair_rs.at[which, source_high], pair
        )

    def lend_copy(which, direction):
        other = piece(which, high * 2 + 1 - low)
        return remote(
            other,
            other,
            lend_ss.at[which, direction],
            lend_rs.at[which],
            below if direction == 0 else above,
        )

    def lend(which):
        pair_arrival(which, high).wait_recv()

        @pl.when(lends_below)
        def _():
            lend_copy(which, 0).start()

        @pl.when(lends_above)
        def _():
            lend_copy(which, 1).start()

    def gathered(which):
        owns[which].wait()
        for source_high in range(half):
            if which in lent:

                @pl.when((high != source_high) & (lender != source_high))
                def _():
                    pair_arrival(which, source_high).wait_recv()

            else:
                pair_arrival(which, source_high).wait_recv()
        if which in lent:
            borrowed = piece(which, lender * 2 + 1 - low)
            remote(
                borrowed, borrowed, lend_ss.at[which, 0], lend_rs.at[which], above
            ).wait_recv()

    chunks = rows // CHUNK
    parts = rows // TILE

    def chunk_rows(chunk):
        return pl.ds(pl.multiple_of(chunk * CHUNK, CHUNK), CHUNK)

    def stream_copy(part):
        at = pl.ds(part * TILE, TILE)
        return remote(
            stream.at[at, :], x.at[at, :], x_ss.at[part], x_rs.at[part], partner
        )

    out_swap = remote(
        g_out.at[:, mine_columns], g_out.at[:, mine_columns], swap_s.at[0], swap_s.at[1], beside
    )

    send_own(0)

    @pl.when(second)
    def _():
        pl.semaphore_wait(go_sem, 1)

    @pl.when(first)
    def _():
        @pl.loop(0, width // TILE)
        def _(tile):
            columns = pl.ds(pl.multiple_of(tile * TILE, TILE), TILE)
            outgoing[:, columns] = jnp.dot(
                select[...], tok[:, columns], preferred_element_type=F32
            ).astype(BF)

        for step in range(1, groups):
            token_copy(step).start()
        own_tokens.start()

    send_own(1)
    for back in range(1, half):
        relay(0, back)
        if back == 1 and 0 in lent:
            lend(0)
    send_own(2)
    for back in range(1, half):
        relay(1, back)
        if back == 1 and 1 in lent:
            lend(1)
    send_own(3)

    @pl.when(first)
    def _():
        for step in range(1, groups):
            token_arrival(step).wait_recv()
        own_tokens.wait()

        @pl.loop(0, width // TILE)
        def _(tile):
            columns = pl.ds(pl.multiple_of(tile * TILE, TILE), TILE)
            x[:, columns] = jnp.dot(
                pick[...], received[:, columns], preferred_element_type=F32
            ).astype(BF)

    relay(2, 1)
    if 2 in lent:
        lend(2)
    gathered(0)
    gathered(1)
    out_swap.start()
    for back in range(2, half):
        relay(2, back)

    @pl.when(second)
    def _():
        for part in range(parts):
            stream_copy(part).wait_recv()

    @pl.loop(0, chunks)
    def _(chunk):
        at = chunk_rows(chunk)
        normed[at, :] = normalised(x[at, :].astype(F32), gain_attn[...].astype(F32)).astype(BF)

    @pl.loop(0, merged.shape[1] // TILE)
    def _(tile):
        columns = pl.ds(pl.multiple_of(tile * TILE, TILE), TILE)
        merged[:, columns] = jnp.dot(normed[...], g_qkv[:, columns], preferred_element_type=F32)

    turns = -(-(half - 1) // chunks)
    lanes = 2 * HEAD_DIM
    lane_of = lax.broadcasted_iota(jnp.int32, (CHUNK, lanes), 1)
    contract = (((1,), (1,)), ((), ()))

    def head_copy(chunk):
        at = chunk_rows(chunk)
        return remote(
            ho_mine.at[at, :], ho_other.at[at, :], ho_ss.at[chunk], ho_rs.at[chunk], beside
        )

    @pl.loop(0, chunks)
    def _(chunk):
        at = chunk_rows(chunk)
        hidden_keys = mask[chunk]
        for two in range(quarter // lanes):
            q = merged[at, two * lanes : (two + 1) * lanes]
            k = merged[at, quarter + two * lanes : quarter + (two + 1) * lanes]
            v = merged[at, 2 * quarter + two * lanes : 2 * quarter + (two + 1) * lanes].astype(BF)
            k_top = k.astype(BF)
            k_rest = (k - k_top.astype(F32)).astype(BF)
            outs = []
            for head in range(2):
                mine = (lane_of < HEAD_DIM) if head == 0 else (lane_of >= HEAD_DIM)
                q_head = jnp.where(mine, q, 0.0)
                q_top = q_head.astype(BF)
                q_rest = (q_head - q_top.astype(F32)).astype(BF)
                scores = (
                    lax.dot_general(q_top, k_top, contract, preferred_element_type=F32)
                    + lax.dot_general(q_top, k_rest, contract, preferred_element_type=F32)
                    + lax.dot_general(q_rest, k_top, contract, preferred_element_type=F32)
                ) * HEAD_DIM ** (-0.5)
                scores = scores + hidden_keys
                scores = scores - jnp.max(scores, axis=-1, keepdims=True)
                powers = jnp.exp(scores)
                total = jnp.sum(powers, axis=-1, keepdims=True)
                mixed = jnp.dot(powers.astype(BF), v, preferred_element_type=F32)
                outs.append(mixed / total)
            ho_mine[at, two * lanes : (two + 1) * lanes] = jnp.where(
                lane_of < HEAD_DIM, outs[0], outs[1]
            ).astype(BF)
        head_copy(chunk).start()
        for turn in range(turns):
            relay(3, chunk * turns + turn + 1)

    @pl.when(first)
    def _():
        pl.semaphore_signal(
            go_sem, inc=1, device_id=partner, device_id_type=pl.DeviceIdType.MESH
        )

    @pl.loop(0, chunks)
    def _(chunk):
        head_copy(chunk).wait()

    out_arrival = g_out.at[:, pl.ds(pl.multiple_of((1 - tensor) * quarter, quarter), quarter)]
    remote(out_arrival, out_arrival, swap_s.at[0], swap_s.at[1], beside).wait_recv()
    mine_rows = pl.ds(pl.multiple_of(tensor * quarter, quarter), quarter)
    other_rows = pl.ds(pl.multiple_of((1 - tensor) * quarter, quarter), quarter)

    @pl.loop(0, width // TILE)
    def _(tile):
        columns = pl.ds(pl.multiple_of(tile * TILE, TILE), TILE)
        mid[:, columns] = (
            x[:, columns].astype(F32)
            + jnp.dot(ho_mine[...], g_out[mine_rows, columns], preferred_element_type=F32)
            + jnp.dot(ho_other[...], g_out[other_rows, columns], preferred_element_type=F32)
        )

    @pl.loop(0, chunks)
    def _(chunk):
        at = chunk_rows(chunk)
        normed[at, :] = normalised(mid[at, :], gain_mlp[...].astype(F32)).astype(BF)

    gathered(2)

    @pl.loop(0, hidden.shape[1] // TILE)
    def _(tile):
        columns = pl.ds(pl.multiple_of(tile * TILE, TILE), TILE)
        raised = (
            jnp.dot(normed[...], g_up[:, columns], preferred_element_type=F32)
            + bias[:, columns].astype(F32)
        )
        hidden[:, columns] = (raised * (1.0 + lax.erf(raised * (0.5**0.5))) * 0.5).astype(BF)

    size_down = w_down.shape[1]

    def partial_copy(number):
        return remote(
            p_mine.at[number], p_other.at[number], p_ss.at[number], p_rs.at[number], beside
        )

    def partial(number):
        if narrow:
            columns_of = g_down[number]
        else:
            columns_of = g_down[:, pl.ds(pl.multiple_of(number * size_down, size_down), size_down)]
        p_mine[number] = jnp.dot(hidden[...], columns_of, preferred_element_type=F32).astype(BF)
        partial_copy(number).start()

    owns[3].wait()

    @pl.loop(0, half)
    def _(source_high):
        partial(source_high * 2 + low)

    @pl.loop(0, half)
    def _(step):
        source_high = jnp.where(in_lower, high + step, high - step + half) % half
        pair_arrival(3, source_high).wait_recv()
        partial(source_high * 2 + 1 - low)

    if narrow:
        joined = TILE // size_down
        tiles = [
            (slice(t * TILE, (t + 1) * TILE), [t * joined + i for i in range(joined)])
            for t in range(width // TILE)
        ]
    else:
        tiles = [
            (slice(t * size_down, (t + 1) * size_down), [t]) for t in range(width // size_down)
        ]
    for number in range(groups):
        partial_copy(number).wait()

    @pl.loop(0, parts)
    def _(part):
        at = pl.ds(pl.multiple_of(part * TILE, TILE), TILE)
        for columns, numbers in tiles:
            added = [
                p_mine[number, at, :].astype(F32) + p_other[number, at, :].astype(F32)
                for number in numbers
            ]
            added = added[0] if len(added) == 1 else jnp.concatenate(added, axis=1)
            stream[at, columns] = (mid[at, columns] + added).astype(BF)

    @pl.when(first)
    def _():
        for part in range(parts):
            stream_copy(part).start()

    result = remote(
        fin.at[:, pl.ds(0, section_rows), :], o_ref, fin_s.at[0], fin_s.at[1], partner
    )

    @pl.when(second)
    def _():
        per = CHUNK // block
        own_columns = pl.ds(pl.multiple_of(tensor * quarter, quarter), quarter)

        @pl.loop(0, chunks)
        def _(chunk):
            at = chunk_rows(chunk)
            values = stream[at, :].astype(F32)
            average = jnp.mean(values, axis=-1, keepdims=True)
            centred = values - average
            scale = lax.rsqrt(jnp.mean(centred * centred, axis=-1, keepdims=True) + epsilon)
            piece_values = (
                (stream[at, own_columns].astype(F32) - average) * scale * gain_final[:, own_columns].astype(F32)
            )
            fin[pl.ds(chunk * per, per)] = piece_values.astype(BF).reshape(per, block, quarter)

        result.start()
        o_ref[...] = fin[:, section_rows:, :]
        result.wait_send()

    @pl.when(first)
    def _():
        for part in range(parts):
            stream_copy(part).wait_send()
        for step in range(1, groups):
            token_copy(step).wait_send()
        result.wait_recv()

    out_swap.wait_send()
    for which in range(4):
        source = sources[which]
        for back in range(half):

            @pl.when(has_above & (high - back >= 0))
            def _():
                up_copy(which, high - back, source).wait_send()

            @pl.when(has_below & (high + back < half))
            def _():
                down_copy(which, high + back, source).wait_send()

            if which in lent:

                @pl.when(lender != back)
                def _():
                    pair_copy(which, back, source).wait_send()

            else:
                pair_copy(which, back, source).wait_send()
        if which in lent:

            @pl.when(lends_below)
            def _():
                lend_copy(which, 0).wait_send()

            @pl.when(lends_above)
            def _():
                lend_copy(which, 1).wait_send()


def local(
    tokens,
    counts,
    assign,
    qkv_weight,
    out_weight,
    up_weight,
    up_bias,
    down_weight,
    attn_gain,
    mlp_gain,
    final_gain,
):
    groups = lax.axis_size("dp")
    sections = lax.axis_size("section")
    tensor_ranks = lax.axis_size("tensor")
    images_dev, block, width = tokens.shape
    quarter = width // tensor_ranks
    capacity = (images_dev + groups - 1) // groups
    total_images = assign.shape[0]
    rows = images_dev * block
    slots = groups * capacity
    my_group = lax.axis_index("dp")
    numbers = jnp.arange(total_images, dtype=jnp.int32)
    matches = (assign[:, None] == numbers[None, :]).astype(jnp.int32)
    slot_of = jnp.sum(matches * numbers[:, None], axis=0)
    target = slot_of // images_dev
    source_group = numbers // images_dev
    earlier = (
        (source_group[:, None] == source_group[None, :])
        & (target[:, None] == target[None, :])
        & (numbers[None, :] < numbers[:, None])
    )
    rank_all = jnp.sum(earlier.astype(jnp.int32), axis=1)
    send_slot = lax.dynamic_slice_in_dim(
        target * capacity + rank_all, my_group * images_dev, images_dev
    )
    my_images = lax.dynamic_slice_in_dim(assign, my_group * images_dev, images_dev)
    chosen = (my_images[:, None] == numbers[None, :]).astype(jnp.int32)
    receive_slot = jnp.sum(chosen * (source_group * capacity + rank_all)[None, :], axis=1)
    live_counts = jnp.sum(chosen * counts[None, :], axis=1)
    within = jnp.tile(jnp.arange(block, dtype=jnp.int32), images_dev)
    buffer_rows = jnp.arange(slots * block, dtype=jnp.int32)
    send_rows = jnp.repeat(send_slot, block) * block + within
    receive_rows = jnp.repeat(receive_slot, block) * block + within
    select = (buffer_rows[:, None] == send_rows[None, :]).astype(BF)
    pick = (buffer_rows[None, :] == receive_rows[:, None]).astype(BF)
    per = CHUNK // block
    key_live = within.reshape(-1, CHUNK) < jnp.repeat(live_counts, block).reshape(-1, CHUNK)
    image_of = jnp.arange(CHUNK) // block
    visible = key_live[:, None, :] & (image_of[:, None] == image_of[None, :])[None]
    mask = jnp.where(visible, 0.0, -1e30).astype(F32)
    w_qkv = qkv_weight[0].reshape(qkv_weight.shape[1], -1)
    w_out, w_up, w_down = out_weight[0], up_weight[0], down_weight[0]
    units = w_up.shape[1]
    down_columns = w_down.shape[1]
    down_shape = (units, width) if down_columns % 128 == 0 else (groups, units, down_columns)
    half = groups // 2
    cap_rows = capacity * block
    vmem = pl.BlockSpec(memory_space=pltpu.VMEM)
    anywhere = pl.BlockSpec(memory_space=pl.ANY)
    dma = pltpu.SemaphoreType.DMA
    section_rows = block // sections
    encoded = pl.pallas_call(
        functools.partial(encoder, groups, cap_rows),
        out_shape=jax.ShapeDtypeStruct((images_dev, section_rows, quarter), BF),
        in_specs=[vmem] * 8 + [anywhere] * 4,
        out_specs=vmem,
        scratch_shapes=[
            pltpu.VMEM((width, w_qkv.shape[1]), BF),
            pltpu.VMEM((width, width), BF),
            pltpu.VMEM((width, units), BF),
            pltpu.VMEM(down_shape, BF),
            pltpu.VMEM((slots * block, width), BF),
            pltpu.VMEM((slots * block, width), BF),
            pltpu.VMEM((rows, width), BF),
            pltpu.VMEM((rows, width), BF),
            pltpu.VMEM((rows, w_qkv.shape[1]), F32),
            pltpu.VMEM((rows, quarter), BF),
            pltpu.VMEM((rows, quarter), BF),
            pltpu.VMEM((rows, width), F32),
            pltpu.VMEM((rows, units), BF),
            pltpu.VMEM((groups, rows, down_columns), BF),
            pltpu.VMEM((groups, rows, down_columns), BF),
            pltpu.VMEM((rows, width), BF),
            pltpu.VMEM((images_dev, block, quarter), BF),
            dma((groups,)),
            dma((groups,)),
            dma((4,)),
            dma((4, half)),
            dma((4, half)),
            dma((4, half)),
            dma((4, half)),
            dma((4, half)),
            dma((rows // CHUNK,)),
            dma((rows // CHUNK,)),
            dma((groups,)),
            dma((groups,)),
            dma((rows // TILE,)),
            dma((rows // TILE,)),
            dma((2,)),
            dma((4, 2)),
            dma((4,)),
            dma((2,)),
            pltpu.SemaphoreType.REGULAR,
        ],
        compiler_params=pltpu.CompilerParams(
            collective_id=0, has_side_effects=True, vmem_limit_bytes=60 * 1024 * 1024
        ),
    )(
        tokens.reshape(rows, width),
        select,
        pick,
        mask,
        up_bias,
        attn_gain,
        mlp_gain,
        final_gain[None],
        w_qkv,
        w_out,
        w_up,
        w_down,
    )
    row_numbers = lax.axis_index("section") * section_rows + jnp.arange(section_rows)
    alive = row_numbers[None, :, None] < live_counts[:, None, None]
    return jnp.where(alive, encoded, jnp.zeros_like(encoded))


def solution(mesh):
    in_specs = (
        P("dp", None, None),
        P(),
        P(),
        P("section", "dp", None, "tensor"),
        P("section", "dp", None),
        P("section", "dp", "tensor"),
        P("section", "tensor"),
        P("section", "tensor", "dp"),
        P("section", None),
        P("section", None),
        P(),
    )
    out_specs = P("dp", "section", "tensor")
    return jax.shard_map(local, mesh=mesh, in_specs=in_specs, out_specs=out_specs, check_vma=False)
```
